512 devices in a mesh: op: 4 (over x), sec: 128 (over z, y, core).
Axes of the slice: x: 4, y: 4, z: 16, core: 2. Of those that a mesh axis runs over, the one named last changes fastest.
Arguments:
- wave: bfloat16 [8192, 8192], P(None, 'sec'), may hold values from -6 to 6
- left_env: bfloat16 [4, 128, 64, 64], P('op', 'sec'), may hold values from -1 to 1
- right_env: bfloat16 [4, 128, 64, 64], P('op', 'sec'), may hold values from -0.5 to 0.5
- left_map: int32 [4, 128], P('op'), may hold values from 0 to 127
- right_map: int32 [4, 128], P('op'), may hold values from 0 to 127
- left_dims: int32 [128], replicated, may hold values from 1 to 64, 6144 in all
- right_dims: int32 [128], replicated, may hold values from 1 to 64, 6144 in all
Outputs:
- product: bfloat16 [8192, 8192], P('sec')
The draws below stay inside these ranges and needn't reach their ends.
Inputs may be any that keep to these rules, and one draw needn't show every extreme that they name: `left_dims`: the sizes sum to 6144 and the largest is exactly 64. `right_dims`: the sizes sum to 6144 and the largest is exactly 64.
All inputs are finite; a program needn't handle non-finite values.
Results may differ from the reference program's by a relative error of at most 0.023.
Values may be sent and summed in bfloat16 or wider, within the bound.
No kernel may reach another device: no remote copies, remote signals or barrier semaphores. Data moves between devices by JAX's collectives and lax.ppermute only.
A program may use at most 64 MiB of HBM per device.

```python
import math
import jax
import jax.numpy as jnp
import numpy as np
from jax import lax

B = 64
TERM_DEV = 1
SECTORS = 128
TERMS = 4
N_OP = 4


def plant(array, own_key, smallest, top_value):
    index_at = [jax.random.randint(jax.random.fold_in(own_key, axis), (), 0, length) for axis, length in enumerate(array.shape)]
    main_axis = array.shape.index(max(array.shape))
    beside = index_at[:main_axis] + [(index_at[main_axis] + 1) % array.shape[main_axis]] + index_at[main_axis + 1:]
    return array.at[tuple(index_at)].set(smallest).at[tuple(beside)].set(top_value)


def shard_levels(own_key, shape, pieces, least, top_value):
    factor_of, own = 1.0, jax.random.fold_in(own_key, 6)
    for dim, shards_of in pieces:
        draws = jnp.exp(jax.random.uniform(jax.random.fold_in(own, dim), (shards_of,), jnp.float32, least / len(pieces), top_value / len(pieces)))
        factor_of = factor_of * jnp.repeat(draws, shape[dim] // shards_of).reshape([-1 if axis == dim else 1 for axis in range(len(shape))])
    return factor_of


def length_profile(amount, total, limit, slope):
    loads = [(1 << 20) // math.isqrt(grade ** slope) + 1 for grade in range(2, amount + 1)]
    rest, holding = total - limit - (amount - 1), [1] * (amount - 1)
    while rest > 0:
        movable = [i for i in range(amount - 1) if holding[i] < limit]
        pool, remaining = sum([loads[i] for i in movable]), rest
        for i in movable:
            more = min(limit - holding[i], max(1, remaining * loads[i] // pool), rest)
            holding[i] = holding[i] + more
            rest = rest - more
    return np.array([limit] + holding)


def uneven(stream_key, number_of, total, bound, lean):
    if number_of == 2:
        one = jax.random.randint(stream_key, (), max(1, total - bound), min(bound, total - 1) + 1)
        return jnp.stack([one, total - one])
    sizes = jnp.asarray(length_profile(number_of, total, bound, lean), jnp.int32)
    pairs = (number_of - 1) // 2
    source_of, receiver = sizes[1:1 + 2 * pairs:2], sizes[2:2 + 2 * pairs:2]
    room = jnp.minimum(source_of - 1, bound - receiver)
    passed = jax.random.randint(jax.random.fold_in(stream_key, 1), (pairs,), 0, 1 << 20) % (room + 1)
    sizes = sizes.at[1:1 + 2 * pairs:2].set(source_of - passed).at[2:2 + 2 * pairs:2].set(receiver + passed)
    return sizes[jax.random.permutation(jax.random.fold_in(stream_key, 2), number_of)]


def gaussian(key, shape, spread, limit, split=(), held_as=jnp.bfloat16):
    drawn = jax.random.normal(key, shape, jnp.float32) * spread
    if len(split) > 0:
        drawn = shard_levels(key, shape, split, -0.22, 0.18) * drawn
    return jnp.clip(drawn, min=-limit, max=limit).astype(held_as)


def setup_inputs(seed: int = 0) -> dict:
    streams_of = jax.random.split(jax.random.key(seed), 8)
    wave = gaussian(streams_of[0], (SECTORS * B, SECTORS * B), 1.0, 6.0, ((1, 128),))
    left_env = gaussian(streams_of[1], (TERMS, SECTORS, B, B), (B // 2) ** -0.5, 1.0, ((0, 4), (1, 128)))
    right_env = gaussian(streams_of[2], (TERMS, SECTORS, B, B), (B * TERMS // 2) ** -0.5, 0.5, ((0, 4), (1, 128)))
    left_map = plant(jax.random.randint(streams_of[3], (TERMS, SECTORS), 0, SECTORS), jax.random.fold_in(streams_of[3], 1), 0, SECTORS - 1).astype(jnp.int32)
    right_map = plant(jax.random.randint(streams_of[4], (TERMS, SECTORS), 0, SECTORS), jax.random.fold_in(streams_of[4], 1), 0, SECTORS - 1).astype(jnp.int32)
    left_dims = uneven(streams_of[5], SECTORS, 3 * SECTORS * B // 4, B, 2).astype(jnp.int32)
    right_dims = uneven(streams_of[6], SECTORS, 3 * SECTORS * B // 4, B, 2).astype(jnp.int32)
    return {"wave": wave, "left_env": left_env, "right_env": right_env, "left_map": left_map, "right_map": right_map, "left_dims": left_dims, "right_dims": right_dims}


def state_mask(extents):
    states = jnp.arange(B, dtype=jnp.int32)
    return (states[None, :] < extents[:, None]).astype(jnp.float32).reshape(-1)


def left_apply(matrix, environment, source):
    blocks = matrix.reshape(SECTORS, B, -1)[source]
    return jnp.einsum('aik,akn->ain', environment.astype(jnp.float32), blocks.astype(jnp.float32)).reshape(SECTORS * B, -1)


def right_apply(matrix, environment, source):
    blocks = matrix.reshape(matrix.shape[0], SECTORS, B)[:, source, :]
    return jnp.einsum('mbk,bkj->mbj', blocks.astype(jnp.float32), environment.astype(jnp.float32)).reshape(matrix.shape[0], -1)


def hamiltonian(matrix, left_env, right_env, left_map, right_map, cell_mask, left_first):
    summed = jnp.zeros(matrix.shape, jnp.float32)
    for group_id in range(N_OP):
        partial_value = jnp.zeros(matrix.shape, jnp.float32)
        for member in range(TERM_DEV):
            term_id = group_id * TERM_DEV + member
            if left_first:
                middle = left_apply(matrix, left_env[term_id], left_map[term_id]).astype(jnp.bfloat16)
                partial_value = partial_value + right_apply(middle, right_env[term_id], right_map[term_id])
            else:
                middle = right_apply(matrix, right_env[term_id], right_map[term_id]).astype(jnp.bfloat16)
                partial_value = partial_value + left_apply(middle, left_env[term_id], left_map[term_id])
        rounded = lax.optimization_barrier(partial_value.astype(jnp.bfloat16))
        summed = summed + rounded.astype(jnp.float32)
    return (summed * cell_mask).astype(jnp.bfloat16)


def reference(wave, left_env, right_env, left_map, right_map, left_dims, right_dims):
    row_mask = state_mask(left_dims)
    col_mask = state_mask(right_dims)
    cell_mask = row_mask[:, None] * col_mask[None, :]
    initial = jnp.where(cell_mask > 0, wave, jnp.zeros_like(wave))
    first_pass = hamiltonian(initial, left_env, right_env, left_map, right_map, cell_mask, True)
    second_pass = hamiltonian(first_pass, left_env, right_env, left_map, right_map, cell_mask, False)
    return hamiltonian(second_pass, left_env, right_env, left_map, right_map, cell_mask, True)
```

```python
import functools

import jax
import jax.numpy as jnp
from jax import lax
from jax.experimental import pallas as pl
from jax.experimental.pallas import tpu as pltpu
from jax.sharding import Mesh
from jax.sharding import PartitionSpec as P

BF16, F32 = jnp.bfloat16, jnp.float32
NT = (((1,), (1,)), ((), ()))
SEC = ("z", "y", "c")
ALL = ("op",) + SEC


def iota(shape, axis):
    return lax.broadcasted_iota(jnp.int32, shape, axis)


def spot(info, sizes, sector):
    nz, ny = sizes
    core, rest = sector & 1, sector >> 1
    return ((core ^ info[2]) * ny + lax.rem(rest, ny)) * nz + lax.div(rest, ny)


def fold_out(out_ref, pair, count, first, second):
    for q in range(4):
        rows = jnp.concatenate([first[8 * q : 8 * q + 8], second[8 * q : 8 * q + 8]], axis=0)
        start = pl.multiple_of(q * count * 8 + pair * 16, 16)
        out_ref[pl.ds(start, 16), :] = rows.astype(BF16)


def left_kernel(count, sizes, info, source, row_dims, col_dims, wave, env, out, blocks):
    lane = iota((64, 128), 1)
    low = lane < 64
    alive = iota((64, 128), 0) < col_dims[info[1]]

    def spread(pair, carry):
        value = wave[:, pl.ds(pl.multiple_of(pair * 128, 128), 128)].astype(F32)
        extent = jnp.where(low, row_dims[2 * pair], row_dims[2 * pair + 1] + 64)
        value = jnp.where(alive & (lane < extent), value, 0.0)
        turned = pltpu.roll(value, 64, 1)
        blocks[2 * pair] = jnp.where(low, value, turned).astype(BF16)
        blocks[2 * pair + 1] = jnp.where(low, turned, value).astype(BF16)
        return carry

    lax.fori_loop(0, count // 2, spread, 0, unroll=2)
    zero = jnp.zeros((64, 128), BF16)

    def product(block):
        place = spot(info, sizes, block)
        e = env[pl.ds(pl.multiple_of(place * 32, 32), 32), :]
        f = blocks[source[block]]
        rhs = jnp.concatenate([jnp.where(low, f, zero), jnp.where(low, zero, f)], axis=0)
        return lax.dot_general(e, rhs, NT, preferred_element_type=F32)

    def step(pair, carry):
        fold_out(out, pair, count, product(2 * pair), product(2 * pair + 1))
        return carry

    lax.fori_loop(0, count // 2, step, 0, unroll=2)


def middle_kernel(
    count, sizes, turn, last, info, source, row_dims, col_dims,
    arrived, env_0, env_1, env_2, env_3, out, env, tiles, held, sems,
):
    copies = [
        pltpu.make_async_copy(ref, env.at[info[3 + i]], sems.at[i])
        for i, ref in enumerate((env_0, env_1, env_2, env_3))
    ]
    for copy in copies:
        copy.start()
    lane8 = iota((16, 128), 1)
    low8 = lane8 < 64
    bit0, bit1 = (lane8 & 8) == 0, (lane8 & 16) == 0

    def place(pair, carry):
        got = [
            arrived[pl.ds(pl.multiple_of(w * count * 8 + pair * 16, 16), 16), :].astype(F32)
            for w in range(4)
        ]
        if turn:
            for a, b in ((0, 1), (2, 3)):
                one, two = got[a], got[b]
                got[a] = jnp.where(bit0, one, pltpu.roll(two, 8, 1))
                got[b] = jnp.where(bit0, pltpu.roll(one, 120, 1), two)
            for a, b in ((0, 2), (1, 3)):
                one, two = got[a], got[b]
                got[a] = jnp.where(bit1, one, pltpu.roll(two, 16, 1))
                got[b] = jnp.where(bit1, pltpu.roll(one, 112, 1), two)
        for w in range(4):
            turned = pltpu.roll(got[w], 64, 1)
            top, bottom = jnp.where(low8, got[w], turned), jnp.where(low8, turned, got[w])
            for k in range(2):
                rows = slice(8 * k, 8 * k + 8)
                tile = jnp.concatenate([top[rows], bottom[rows]], axis=0)
                tiles[w, 2 * pair + k] = tile.astype(BF16)
        return carry

    lax.fori_loop(0, count // 2, place, 0, unroll=2)
    for copy in copies:
        copy.wait()

    low = iota((16, 128), 1) < 64
    upper = iota((16, 128), 0) < 8
    zero = jnp.zeros((16, 128), BF16)
    pad = jnp.zeros((32, 96), F32)
    row = iota((16, 128), 0)
    natural = (row & 7) + (row >> 3) * 32 + info[0] * 8
    row_alive = natural < row_dims[info[1]]
    lane_in = iota((16, 128), 1) & 63

    def env_of(block):
        start = pl.multiple_of(spot(info, sizes, block) * 32, 32)
        return jnp.concatenate([env[w, pl.ds(start, 32), :] for w in range(4)], axis=1)

    def summed(block):
        lhs = []
        for w in range(4):
            t = tiles[w, source[w, block]]
            lhs.append(jnp.concatenate([jnp.where(low, t, zero), jnp.where(low, zero, t)], axis=0))
        lhs = jnp.concatenate(lhs, axis=1)
        total = lax.dot_general(lhs, env_of(block), NT, preferred_element_type=F32)
        total = jnp.concatenate([total, pad], axis=1)
        total = total[:16] + pltpu.roll(total[16:], 32, 1)
        return jnp.where(row_alive & (lane_in < col_dims[block]), total, 0.0)

    if last:

        def finish(pair, carry):
            value = summed(2 * pair) + pltpu.roll(summed(2 * pair + 1), 64, 1)
            out[:, pl.ds(pl.multiple_of(pair * 128, 128), 128)] = value.astype(BF16)
            return carry

        lax.fori_loop(0, count // 2, finish, 0, unroll=2)
        return

    def keep(block, carry):
        value = summed(block)
        value = value + pltpu.roll(value, 64, 1)
        first, second = value[:8], value[8:]
        held[block] = jnp.concatenate([first, first, second, second], axis=0).astype(BF16)
        return carry

    lax.fori_loop(0, count, keep, 0, unroll=4)
    masks = [[(upper if p == 0 else ~upper) & (low if h == 0 else ~low) for h in range(2)] for p in range(2)]

    def product(block):
        slots = []
        for w in range(4):
            both = held[source[w, block]]
            rows = []
            for h in range(2):
                for half in range(2):
                    tile = jnp.where(masks[w & 1][h], both[16 * half : 16 * half + 16], zero)
                    rows += [tile, zero] if w < 2 else [zero, tile]
            slots.append(jnp.concatenate(rows, axis=0))
        rhs = jnp.concatenate(slots, axis=1)
        return lax.dot_general(env_of(block), rhs, NT, preferred_element_type=F32)

    def step(pair, carry):
        fold_out(out, pair, count, product(2 * pair), product(2 * pair + 1))
        return carry

    lax.fori_loop(0, count // 2, step, 0, unroll=2)


SMEM = pl.BlockSpec(memory_space=pltpu.SMEM)
VMEM = pl.BlockSpec(memory_space=pltpu.VMEM)
ANY = pl.BlockSpec(memory_space=pl.ANY)


def left_stage(count, sizes, info, source, row_dims, col_dims, wave, env):
    return pl.pallas_call(
        functools.partial(left_kernel, count, sizes),
        out_shape=jax.ShapeDtypeStruct((count * 32, 128), BF16),
        in_specs=[SMEM] * 4 + [VMEM] * 2,
        out_specs=VMEM,
        scratch_shapes=[pltpu.VMEM((count, 64, 128), BF16)],
        cost_estimate=pl.CostEstimate(flops=count * 2**20, bytes_accessed=count * 24576, transcendentals=0),
        name="left_stage",
    )(info, source, row_dims, col_dims, wave, env)


def middle_stage(count, sizes, turn, last, info, source, row_dims, col_dims, arrived, envs):
    shape = (16, count * 64) if last else (count * 32, 128)
    return pl.pallas_call(
        functools.partial(middle_kernel, count, sizes, turn, last),
        out_shape=jax.ShapeDtypeStruct(shape, BF16),
        in_specs=[SMEM] * 4 + [VMEM] + [ANY] * 4,
        out_specs=VMEM,
        scratch_shapes=[
            pltpu.VMEM((4, count * 32, 128), BF16),
            pltpu.VMEM((4, count, 16, 128), BF16),
            pltpu.VMEM((count, 32, 128), BF16),
            pltpu.SemaphoreType.DMA((4,)),
        ],
        cost_estimate=pl.CostEstimate(flops=count * 2**23, bytes_accessed=count * 49152, transcendentals=0),
        name="last_stage" if last else "middle_stage",
    )(info, source, row_dims, col_dims, arrived, *envs)


def fold(block):
    return jnp.concatenate([block[:32], block[32:]], axis=1)


def copies_to(value, axis, size):
    return lax.all_to_all(jnp.broadcast_to(value, (size,) + value.shape), axis, 0, 0, tiled=True)


def exchange(chunks, devices):
    shape = chunks.shape
    return lax.all_to_all(chunks.reshape(devices, 8, 128), ALL, 0, 0, tiled=True).reshape(shape)


def on_device(sizes, wave, left_env, right_env, left_map, right_map, left_dims, right_dims):
    nz, ny = sizes
    count = left_map.shape[1]
    me, core = lax.axis_index("op"), lax.axis_index("c")
    sector = lax.axis_index(SEC)
    shifts = (0, 1, 3, 2)
    info = jnp.stack([me, sector, core] + [lax.rem(me + 4 - s, 4) for s in shifts] + [me]).astype(jnp.int32)

    maps = copies_to(jnp.stack([left_map[0], right_map[0]]), "op", 4)
    own = jnp.stack([fold(left_env[0, 0]), fold(right_env[0, 0].T)])
    over_z = copies_to(own, "z", nz)
    over_y = copies_to(over_z, "y", ny)
    other = lax.ppermute(over_y, "c", [(0, 1), (1, 0)])

    def gathered(which):
        both = jnp.stack([over_y[:, :, which], other[:, :, which]])
        return both.reshape(count * 32, 128)

    left_own, right_own = gathered(0), gathered(1)

    def over_op(value):
        moved = [lax.ppermute(value, "op", [(i, (i + s) % 4) for i in range(4)]) for s in shifts[1:]]
        return [value] + moved

    chunks = left_stage(count, sizes, info, left_map[0], left_dims, right_dims, wave.T, left_own)
    rights = over_op(right_own)
    arrived = exchange(chunks, 4 * count)
    left_late, arrived = lax.optimization_barrier((left_own, arrived))
    chunks = middle_stage(
        count, sizes, False, False, info, maps[:, 1], left_dims, right_dims, arrived, rights
    )
    lefts = over_op(left_late)
    arrived = exchange(chunks, 4 * count)
    chunks = middle_stage(
        count, sizes, True, False, info, maps[:, 0], right_dims, left_dims, arrived, lefts
    )
    arrived = exchange(chunks, 4 * count)
    piece = middle_stage(
        count, sizes, True, True, info, maps[:, 1], left_dims, right_dims, arrived, rights
    )
    pieces = copies_to(piece, "op", 4)
    return pieces.reshape(4, 2, 8, count * 64).swapaxes(0, 1).reshape(64, count * 64)


def solution(mesh):
    n_op, n_sec = mesh.devices.shape
    ny = 4
    nz = n_sec // (2 * ny)
    split = Mesh(mesh.devices.reshape(n_op, nz, ny, 2), ALL)
    placed = (
        P(None, SEC),
        P("op", SEC, None, None),
        P("op", SEC, None, None),
        P("op", None),
        P("op", None),
        P(),
        P(),
    )
    return jax.shard_map(
        functools.partial(on_device, (nz, ny)),
        mesh=split, in_specs=placed, out_specs=P(SEC, None), check_vma=False,
    )
```

```python
import functools

import jax
import jax.numpy as jnp
from jax import lax
from jax.experimental import pallas as pl
from jax.experimental.pallas import tpu as pltpu
from jax.sharding import Mesh
from jax.sharding import PartitionSpec as P

BF16, F32 = jnp.bfloat16, jnp.float32
NT = (((1,), (1,)), ((), ()))
SEC = ("z", "y", "c")
ALL = ("op",) + SEC


def iota(shape, axis):
    return lax.broadcasted_iota(jnp.int32, shape, axis)


def spot(info, sizes, sector):
    nz, ny = sizes
    core, rest = sector & 1, sector >> 1
    return ((core ^ info[2]) * ny + (rest & (ny - 1))) * nz + (rest >> (ny.bit_length() - 1))


def fold_out(out_ref, pair, count, first, second):
    for q in range(4):
        rows = jnp.concatenate([first[8 * q : 8 * q + 8], second[8 * q : 8 * q + 8]], axis=0)
        start = pl.multiple_of(q * count * 8 + pair * 16, 16)
        out_ref[pl.ds(start, 16), :] = rows.astype(BF16)


def left_kernel(count, sizes, info, source, row_dims, col_dims, wave, env, out, blocks):
    lane = iota((64, 128), 1)
    low = lane < 64
    alive = iota((64, 128), 0) < col_dims[info[1]]

    def spread(pair, carry):
        value = wave[:, pl.ds(pl.multiple_of(pair * 128, 128), 128)].astype(F32)
        extent = jnp.where(low, row_dims[2 * pair], row_dims[2 * pair + 1] + 64)
        value = jnp.where(alive & (lane < extent), value, 0.0)
        turned = pltpu.roll(value, 64, 1)
        blocks[2 * pair] = jnp.where(low, value, turned).astype(BF16)
        blocks[2 * pair + 1] = jnp.where(low, turned, value).astype(BF16)
        return carry

    lax.fori_loop(0, count // 2, spread, 0, unroll=16)
    zero = jnp.zeros((64, 128), BF16)

    def product(block):
        place = spot(info, sizes, block)
        e = env[pl.ds(pl.multiple_of(place * 32, 32), 32), :]
        f = blocks[source[block]]
        rhs = jnp.concatenate([jnp.where(low, f, zero), jnp.where(low, zero, f)], axis=0)
        return lax.dot_general(e, rhs, NT, preferred_element_type=F32)

    def step(pair, carry):
        fold_out(out, pair, count, product(2 * pair), product(2 * pair + 1))
        return carry

    lax.fori_loop(0, count // 2, step, 0, unroll=16)


def middle_kernel(
    count, sizes, turn, last, info, source, row_dims, col_dims,
    arrived, env_0, env_1, env_2, env_3, out, env, tiles, held, sems,
):
    copies = [
        pltpu.make_async_copy(ref, env.at[info[3 + i]], sems.at[i])
        for i, ref in enumerate((env_0, env_1, env_2, env_3))
    ]
    for copy in copies:
        copy.start()
    lane8 = iota((16, 128), 1)
    low8 = lane8 < 64
    bit0, bit1 = (lane8 & 8) == 0, (lane8 & 16) == 0

    def place(pair, carry):
        got = [
            arrived[pl.ds(pl.multiple_of(w * count * 8 + pair * 16, 16), 16), :].astype(F32)
            for w in range(4)
        ]
        if turn:
            for a, b in ((0, 1), (2, 3)):
                one, two = got[a], got[b]
                got[a] = jnp.where(bit0, one, pltpu.roll(two, 8, 1))
                got[b] = jnp.where(bit0, pltpu.roll(one, 120, 1), two)
            for a, b in ((0, 2), (1, 3)):
                one, two = got[a], got[b]
                got[a] = jnp.where(bit1, one, pltpu.roll(two, 16, 1))
                got[b] = jnp.where(bit1, pltpu.roll(one, 112, 1), two)
        for w in range(4):
            turned = pltpu.roll(got[w], 64, 1)
            top, bottom = jnp.where(low8, got[w], turned), jnp.where(low8, turned, got[w])
            for k in range(2):
                rows = slice(8 * k, 8 * k + 8)
                tile = jnp.concatenate([top[rows], bottom[rows]], axis=0)
                tiles[w, 2 * pair + k] = tile.astype(BF16)
        return carry

    lax.fori_loop(0, count // 2, place, 0, unroll=16)
    for copy in copies:
        copy.wait()

    low = iota((16, 128), 1) < 64
    upper = iota((16, 128), 0) < 8
    zero = jnp.zeros((16, 128), BF16)
    pad = jnp.zeros((32, 96), F32)
    row = iota((16, 128), 0)
    natural = (row & 7) + (row >> 3) * 32 + info[0] * 8
    row_alive = natural < row_dims[info[1]]
    lane_in = iota((16, 128), 1) & 63

    def env_of(block):
        start = pl.multiple_of(spot(info, sizes, block) * 32, 32)
        return jnp.concatenate([env[w, pl.ds(start, 32), :] for w in range(4)], axis=1)

    def summed(block):
        lhs = []
        for w in range(4):
            t = tiles[w, source[w, block]]
            lhs.append(jnp.concatenate([jnp.where(low, t, zero), jnp.where(low, zero, t)], axis=0))
        lhs = jnp.concatenate(lhs, axis=1)
        total = lax.dot_general(lhs, env_of(block), NT, preferred_element_type=F32)
        total = jnp.concatenate([total, pad], axis=1)
        total = total[:16] + pltpu.roll(total[16:], 32, 1)
        return jnp.where(row_alive & (lane_in < col_dims[block]), total, 0.0)

    if last:

        def finish(pair, carry):
            value = summed(2 * pair) + pltpu.roll(summed(2 * pair + 1), 64, 1)
            out[:, pl.ds(pl.multiple_of(pair * 128, 128), 128)] = value.astype(BF16)
            return carry

        lax.fori_loop(0, count // 2, finish, 0, unroll=16)
        return

    def keep(block, carry):
        value = summed(block)
        value = value + pltpu.roll(value, 64, 1)
        first, second = value[:8], value[8:]
        held[block] = jnp.concatenate([first, first, second, second], axis=0).astype(BF16)
        return carry

    lax.fori_loop(0, count, keep, 0, unroll=32)
    masks = [[(upper if p == 0 else ~upper) & (low if h == 0 else ~low) for h in range(2)] for p in range(2)]

    def product(block):
        slots = []
        for w in range(4):
            both = held[source[w, block]]
            rows = []
            for h in range(2):
                for half in range(2):
                    tile = jnp.where(masks[w & 1][h], both[16 * half : 16 * half + 16], zero)
                    rows += [tile, zero] if w < 2 else [zero, tile]
            slots.append(jnp.concatenate(rows, axis=0))
        rhs = jnp.concatenate(slots, axis=1)
        return lax.dot_general(env_of(block), rhs, NT, preferred_element_type=F32)

    def step(pair, carry):
        fold_out(out, pair, count, product(2 * pair), product(2 * pair + 1))
        return carry

    lax.fori_loop(0, count // 2, step, 0, unroll=16)


SMEM = pl.BlockSpec(memory_space=pltpu.SMEM)
VMEM = pl.BlockSpec(memory_space=pltpu.VMEM)
ANY = pl.BlockSpec(memory_space=pl.ANY)


def left_stage(count, sizes, info, source, row_dims, col_dims, wave, env):
    return pl.pallas_call(
        functools.partial(left_kernel, count, sizes),
        out_shape=jax.ShapeDtypeStruct((count * 32, 128), BF16),
        in_specs=[SMEM] * 4 + [VMEM] * 2,
        out_specs=VMEM,
        scratch_shapes=[pltpu.VMEM((count, 64, 128), BF16)],
        compiler_params=pltpu.CompilerParams(vmem_limit_bytes=16 * 2**20),
        cost_estimate=pl.CostEstimate(flops=count * 2**20, bytes_accessed=count * 24576, transcendentals=0),
        name="left_stage",
    )(info, source, row_dims, col_dims, wave, env)


def middle_stage(count, sizes, turn, last, info, source, row_dims, col_dims, arrived, envs):
    shape = (16, count * 64) if last else (count * 32, 128)
    return pl.pallas_call(
        functools.partial(middle_kernel, count, sizes, turn, last),
        out_shape=jax.ShapeDtypeStruct(shape, BF16),
        in_specs=[SMEM] * 4 + [VMEM] + [ANY] * 4,
        out_specs=VMEM,
        scratch_shapes=[
            pltpu.VMEM((4, count * 32, 128), BF16),
            pltpu.VMEM((4, count, 16, 128), BF16),
            pltpu.VMEM((count, 32, 128), BF16),
            pltpu.SemaphoreType.DMA((4,)),
        ],
        compiler_params=pltpu.CompilerParams(vmem_limit_bytes=24 * 2**20),
        cost_estimate=pl.CostEstimate(flops=count * 2**23, bytes_accessed=count * 49152, transcendentals=0),
        name="last_stage" if last else "middle_stage",
    )(info, source, row_dims, col_dims, arrived, *envs)


def fold(block):
    return jnp.concatenate([block[:32], block[32:]], axis=1)


def copies_to(value, axis, size):
    return lax.all_to_all(jnp.broadcast_to(value, (size,) + value.shape), axis, 0, 0, tiled=True)


def exchange(chunks, devices):
    shape = chunks.shape
    return lax.all_to_all(chunks.reshape(devices, 8, 128), ALL, 0, 0, tiled=True).reshape(shape)


def on_device(sizes, wave, left_env, right_env, left_map, right_map, left_dims, right_dims):
    nz, ny = sizes
    count = left_map.shape[1]
    me, core = lax.axis_index("op"), lax.axis_index("c")
    sector = lax.axis_index(SEC)
    shifts = (0, 1, 3, 2)
    info = jnp.stack([me, sector, core] + [lax.rem(me + 4 - s, 4) for s in shifts] + [me]).astype(jnp.int32)

    maps = copies_to(jnp.stack([left_map[0], right_map[0]]), "op", 4)
    own = jnp.stack([fold(left_env[0, 0]), fold(right_env[0, 0].T)])
    over_z = copies_to(own, "z", nz)
    over_y = copies_to(over_z, "y", ny)
    other = lax.ppermute(over_y, "c", [(0, 1), (1, 0)])

    def gathered(which):
        both = jnp.stack([over_y[:, :, which], other[:, :, which]])
        return both.reshape(count * 32, 128)

    left_own, right_own = gathered(0), gathered(1)

    def over_op(value):
        moved = [lax.ppermute(value, "op", [(i, (i + s) % 4) for i in range(4)]) for s in shifts[1:]]
        return [value] + moved

    chunks = left_stage(count, sizes, info, left_map[0], left_dims, right_dims, wave.T, left_own)
    rights = over_op(right_own)
    arrived = exchange(chunks, 4 * count)
    left_late, arrived = lax.optimization_barrier((left_own, arrived))
    chunks = middle_stage(
        count, sizes, False, False, info, maps[:, 1], left_dims, right_dims, arrived, rights
    )
    lefts = over_op(left_late)
    arrived = exchange(chunks, 4 * count)
    chunks = middle_stage(
        count, sizes, True, False, info, maps[:, 0], right_dims, left_dims, arrived, lefts
    )
    arrived = exchange(chunks, 4 * count)
    piece = middle_stage(
        count, sizes, True, True, info, maps[:, 1], left_dims, right_dims, arrived, rights
    )
    pieces = copies_to(piece, "op", 4)
    return pieces.reshape(4, 2, 8, count * 64).swapaxes(0, 1).reshape(64, count * 64)


def solution(mesh):
    n_op, n_sec = mesh.devices.shape
    ny = 4
    nz = n_sec // (2 * ny)
    split = Mesh(mesh.devices.reshape(n_op, nz, ny, 2), ALL)
    placed = (
        P(None, SEC),
        P("op", SEC, None, None),
        P("op", SEC, None, None),
        P("op", None),
        P("op", None),
        P(),
        P(),
    )
    return jax.shard_map(
        functools.partial(on_device, (nz, ny)),
        mesh=split, in_specs=placed, out_specs=P(SEC, None), check_vma=False,
    )
```

```python
import functools

import jax
import jax.numpy as jnp
from jax import lax
from jax.experimental import pallas as pl
from jax.experimental.pallas import tpu as pltpu
from jax.sharding import Mesh
from jax.sharding import PartitionSpec as P

BF16, F32 = jnp.bfloat16, jnp.float32
NT = (((1,), (1,)), ((), ()))
SEC = ("z", "y", "c")
ALL = ("op",) + SEC


def iota(shape, axis):
    return lax.broadcasted_iota(jnp.int32, shape, axis)


def spot(info, sizes, sector):
    nz, ny = sizes
    core, rest = sector & 1, sector >> 1
    return ((core ^ info[2]) * ny + (rest & (ny - 1))) * nz + (rest >> (ny.bit_length() - 1))


def fold_out(out_ref, pair, count, first, second):
    for q in range(4):
        rows = jnp.concatenate([first[8 * q : 8 * q + 8], second[8 * q : 8 * q + 8]], axis=0)
        start = pl.multiple_of(q * count * 8 + pair * 16, 16)
        out_ref[pl.ds(start, 16), :] = rows.astype(BF16)


def pack(dense, start, value):
    dense[pl.ds(start, 32), :] = value
    dense[pl.ds(start + 32, 32), :] = pltpu.roll(value, 64, 1)


def send_packed(dense, out, owners):
    low = iota((16, 128), 1) < 64

    def narrow(step, carry):
        start = pl.multiple_of(step * 16, 16)
        even = dense[pl.ds(start * 2, 16, stride=2), :]
        odd = pltpu.roll(dense[pl.ds(start * 2 + 1, 16, stride=2), :], 64, 1)
        out[pl.ds(start, 16), :] = jnp.where(low, even, odd).astype(BF16)
        return carry

    lax.fori_loop(0, owners * 6 // 16, narrow, 0, unroll=16 if owners > 32 else 1)


def left_kernel(
    count, sizes, info, source, row_dims, col_dims, row_at, wave, env, out, blocks, dense
):
    lane = iota((64, 128), 1)
    low = lane < 64
    alive = iota((64, 128), 0) < col_dims[info[1]]

    def spread(pair, carry):
        value = wave[:, pl.ds(pl.multiple_of(pair * 128, 128), 128)].astype(F32)
        extent = jnp.where(low, row_dims[2 * pair], row_dims[2 * pair + 1] + 64)
        value = jnp.where(alive & (lane < extent), value, 0.0)
        turned = pltpu.roll(value, 64, 1)
        blocks[2 * pair] = jnp.where(low, value, turned).astype(BF16)
        blocks[2 * pair + 1] = jnp.where(low, turned, value).astype(BF16)
        return carry

    lax.fori_loop(0, count // 2, spread, 0, unroll=min(16, count // 2))
    zero = jnp.zeros((64, 128), BF16)

    def product(block):
        place = spot(info, sizes, block)
        e = env[pl.ds(pl.multiple_of(place * 32, 32), 32), :]
        f = blocks[source[block]]
        rhs = jnp.concatenate([jnp.where(low, f, zero), jnp.where(low, zero, f)], axis=0)
        return lax.dot_general(e, rhs, NT, preferred_element_type=F32)

    def group(step, carry):
        values = [product(step * 8 + i) for i in range(8)]
        for i in range(8):
            pack(dense, row_at[step * 8 + i], values[i])
        return carry

    lax.fori_loop(0, count // 8, group, 0, unroll=min(8, count // 8))
    send_packed(dense, out, count * 4)


def middle_kernel(
    count, sizes, turn, last, info, source, row_dims, col_dims, col_at,
    arrived, env_0, env_1, env_3, env_2a, env_2b, out, env, tiles, held, wide, dense, padded, offsets, sems,
):
    half_env = count * 16
    copies = [
        pltpu.make_async_copy(env_0, env.at[info[3]], sems.at[0]),
        pltpu.make_async_copy(env_1, env.at[info[4]], sems.at[1]),
        pltpu.make_async_copy(env_3, env.at[info[5]], sems.at[2]),
        pltpu.make_async_copy(env_2a, env.at[info[6], pl.ds(0, half_env)], sems.at[3]),
        pltpu.make_async_copy(env_2b, env.at[info[6], pl.ds(half_env, half_env)], sems.at[4]),
    ]
    for copy in copies:
        copy.start()
    lane8 = iota((8, 128), 1)
    low8 = lane8 < 64
    rows_in = 8 if last else 6
    total_rows = arrived.shape[0]

    def widen(step, carry):
        start = pl.multiple_of(step * 16, 16)
        wide[pl.ds(start, 16), :] = arrived[pl.ds(start, 16), :].astype(F32)
        return carry

    lax.fori_loop(0, total_rows // 16, widen, 0, unroll=16 if count > 8 else 1)
    wide[pl.ds(total_rows, 8), :] = jnp.zeros((8, 128), F32)


    def settle(w, block, value):
        turned = pltpu.roll(value, 64, 1)
        first, second = jnp.where(low8, value, turned), jnp.where(low8, turned, value)
        tiles[w, block] = jnp.concatenate([first, second], axis=0).astype(BF16)

    if turn:
        bit0, bit1 = (lane8 & 16) == 0, (lane8 & 32) == 0
        zero_tile = jnp.zeros((16, 128), BF16)
        for w in range(4):
            padded[w, count // 2] = zero_tile
        spot_of = iota((256, 128), 0)
        number = (spot_of >> 4) * 12 + (spot_of & 7) * 2 + ((spot_of >> 3) & 1)
        offsets[...] = jnp.where((spot_of & 7) < 6, number, -4096) - (iota((256, 128), 1) & 63)

        def regroup(e, carry):
            sets = []
            for k in range(2):
                got = [wide[pl.ds((8 * e + 4 * k + x) * rows_in, 8), :] for x in range(4)]
                for a, b in ((0, 1), (2, 3)):
                    one, two = got[a], got[b]
                    got[a] = jnp.where(bit0, one, pltpu.roll(two, 16, 1))
                    got[b] = jnp.where(bit0, pltpu.roll(one, 112, 1), two)
                for a, b in ((0, 2), (1, 3)):
                    one, two = got[a], got[b]
                    got[a] = jnp.where(bit1, one, pltpu.roll(two, 32, 1))
                    got[b] = jnp.where(bit1, pltpu.roll(one, 96, 1), two)
                sets.append(got)
            for w in range(4):
                one, two = sets[0][w], sets[1][w]
                first = jnp.where(low8, one, pltpu.roll(two, 64, 1))
                second = jnp.where(low8, pltpu.roll(one, 64, 1), two)
                padded[w, e] = jnp.concatenate([first, second], axis=0).astype(BF16)
            return carry

        lax.fori_loop(0, count // 2, regroup, 0, unroll=min(8, count // 2))
        lane_k = iota((256, 128), 1) & 63

        def place(block, carry):
            at = col_at[block]
            f = lax.div(at, 96)
            pick = (offsets[...] == at - f * 96) & (lane_k < col_dims[block])
            pick = jnp.where(pick, 1.0, 0.0).astype(BF16)
            lhs = [jnp.concatenate([padded[w, f], padded[w, f + 1]], axis=1) for w in range(4)]
            lhs = jnp.concatenate(lhs, axis=0)
            value = jnp.dot(lhs, pick, preferred_element_type=F32).astype(BF16)
            for w in range(4):
                tiles[w, block] = value[16 * w : 16 * w + 16]
            return carry
    else:

        def place(block, carry):
            for w in range(4):
                settle(w, block, wide[pl.ds((w * count + block) * rows_in, 8), :])
            return carry

    lax.fori_loop(0, count, place, 0, unroll=min(16, count))
    for copy in copies:
        copy.wait()

    low = iota((16, 128), 1) < 64
    zero = jnp.zeros((16, 128), BF16)
    pad = jnp.zeros((32, 96), F32)
    lane_in = iota((16, 128), 1) & 63
    if last:
        row = iota((16, 128), 0)
        natural = (row & 7) + (row >> 3) * 32 + info[0] * 8
        row_alive = natural < row_dims[info[1]]

    def env_of(block):
        start = pl.multiple_of(spot(info, sizes, block) * 32, 32)
        return jnp.concatenate([env[w, pl.ds(start, 32), :] for w in range(4)], axis=1)

    def summed(block):
        lhs = []
        for w in range(4):
            t = tiles[w, source[w, block]]
            lhs.append(jnp.concatenate([jnp.where(low, t, zero), jnp.where(low, zero, t)], axis=0))
        lhs = jnp.concatenate(lhs, axis=1)
        total = lax.dot_general(lhs, env_of(block), NT, preferred_element_type=F32)
        total = jnp.concatenate([total, pad], axis=1)
        total = total[:16] + pltpu.roll(total[16:], 32, 1)
        alive = lane_in < col_dims[block]
        return jnp.where(row_alive & alive if last else alive, total, 0.0)

    if last:

        def finish(pair, carry):
            value = summed(2 * pair) + pltpu.roll(summed(2 * pair + 1), 64, 1)
            out[:, pl.ds(pl.multiple_of(pair * 128, 128), 128)] = value.astype(BF16)
            return carry

        lax.fori_loop(0, count // 2, finish, 0, unroll=min(16, count // 2))
        return

    def keep(block, carry):
        value = summed(block)
        held[block] = (value + pltpu.roll(value, 64, 1)).astype(BF16)
        return carry

    lax.fori_loop(0, count, keep, 0, unroll=min(32, count))

    def product(block):
        slots = []
        for w in range(4):
            both = held[source[w, block]]
            rows = []
            for h in range(2):
                tile = jnp.where(low, both, zero) if h == 0 else jnp.where(low, zero, both)
                rows += [tile if v == w else zero for v in range(4)]
            slots.append(jnp.concatenate(rows, axis=0))
        rhs = jnp.concatenate(slots, axis=1)
        return lax.dot_general(env_of(block), rhs, NT, preferred_element_type=F32)

    if turn:

        def step(pair, carry):
            fold_out(out, pair, count, product(2 * pair), product(2 * pair + 1))
            return carry

        lax.fori_loop(0, count // 2, step, 0, unroll=min(16, count // 2))
        return

    def group(step, carry):
        values = [product(step * 8 + i) for i in range(8)]
        for i in range(8):
            pack(dense, col_at[step * 8 + i], values[i])
        return carry

    lax.fori_loop(0, count // 8, group, 0, unroll=min(8, count // 8))
    send_packed(dense, out, count * 4)


SMEM = pl.BlockSpec(memory_space=pltpu.SMEM)
VMEM = pl.BlockSpec(memory_space=pltpu.VMEM)
ANY = pl.BlockSpec(memory_space=pl.ANY)


def left_stage(count, sizes, info, source, row_dims, col_dims, row_at, wave, env):
    return pl.pallas_call(
        functools.partial(left_kernel, count, sizes),
        out_shape=jax.ShapeDtypeStruct((count * 24, 128), BF16),
        in_specs=[SMEM] * 5 + [VMEM] * 2,
        out_specs=VMEM,
        scratch_shapes=[
            pltpu.VMEM((count, 64, 128), BF16),
            pltpu.VMEM((count * 48 + 64, 128), F32),
        ],
        compiler_params=pltpu.CompilerParams(vmem_limit_bytes=20 * 2**20),
        cost_estimate=pl.CostEstimate(flops=count * 2**20, bytes_accessed=count * 24576, transcendentals=0),
        name="left_stage",
    )(info, source, row_dims, col_dims, row_at, wave, env)


def middle_stage(count, sizes, turn, last, info, source, row_dims, col_dims, col_at, arrived, envs):
    shape = (16, count * 64) if last else (count * (32 if turn else 24), 128)
    return pl.pallas_call(
        functools.partial(middle_kernel, count, sizes, turn, last),
        out_shape=jax.ShapeDtypeStruct(shape, BF16),
        in_specs=[SMEM] * 5 + [VMEM] + [ANY] * 5,
        out_specs=VMEM,
        scratch_shapes=[
            pltpu.VMEM((4, count * 32, 128), BF16),
            pltpu.VMEM((4, count, 16, 128), BF16),
            pltpu.VMEM((count, 16, 128), BF16),
            pltpu.VMEM((count * 32 + 8, 128), F32),
            pltpu.VMEM((count * 48 + 64, 128), F32),
            pltpu.VMEM((4, count // 2 + 1, 16, 128), BF16),
            pltpu.VMEM((256, 128), jnp.int32),
            pltpu.SemaphoreType.DMA((5,)),
        ],
        compiler_params=pltpu.CompilerParams(vmem_limit_bytes=26 * 2**20),
        cost_estimate=pl.CostEstimate(flops=count * 2**23, bytes_accessed=count * 49152, transcendentals=0),
        name="last_stage" if last else "middle_stage",
    )(info, source, row_dims, col_dims, col_at, arrived, *envs)


def fold(block):
    return jnp.concatenate([block[:32], block[32:]], axis=1)


def copies_to(value, axis, size):
    return lax.all_to_all(jnp.broadcast_to(value, (size,) + value.shape), axis, 0, 0, tiled=True)


def exchange(chunks, devices):
    shape = chunks.shape
    pieces = chunks.reshape(devices, shape[0] // devices // 2, 2, 128)
    return lax.all_to_all(pieces, ALL, 0, 0, tiled=True).reshape(shape)


def on_device(sizes, wave, left_env, right_env, left_map, right_map, left_dims, right_dims):
    nz, ny = sizes
    count = left_map.shape[1]
    me, core = lax.axis_index("op"), lax.axis_index("c")
    sector = lax.axis_index(SEC)
    shifts = (0, 1, 3, 2)
    starts = [jnp.cumsum(d) - d for d in (left_dims, right_dims)]
    info = jnp.stack([me, sector, core] + [lax.rem(me + 4 - s, 4) for s in shifts] + [me]).astype(jnp.int32)

    maps = copies_to(jnp.stack([left_map[0], right_map[0]]), "op", 4)
    own = jnp.stack([fold(left_env[0, 0]), fold(right_env[0, 0].T)])
    over_z = copies_to(own, "z", nz)
    over_y = copies_to(over_z, "y", ny)
    other = lax.ppermute(over_y, "c", [(0, 1), (1, 0)])

    def gathered(which):
        both = jnp.stack([over_y[:, :, which], other[:, :, which]])
        return both.reshape(count * 32, 128)

    left_own, right_own = gathered(0), gathered(1)

    def over_op(value):
        half = count * 16
        ahead = lax.ppermute(value, "op", [(i, (i + 1) % 4) for i in range(4)])
        behind = lax.ppermute(value, "op", [(i, (i + 3) % 4) for i in range(4)])
        far_a = lax.ppermute(ahead[:half], "op", [(i, (i + 1) % 4) for i in range(4)])
        far_b = lax.ppermute(behind[half:], "op", [(i, (i + 3) % 4) for i in range(4)])
        return [value, ahead, behind, far_a, far_b]

    stage = functools.partial(middle_stage, count, sizes)
    rows, cols = (left_dims, right_dims, starts[1]), (right_dims, left_dims, starts[0])
    chunks = left_stage(
        count, sizes, info, left_map[0], left_dims, right_dims, starts[0], wave.T, left_own
    )
    rights = over_op(right_own)
    arrived = exchange(chunks, 4 * count)
    left_late, arrived = lax.optimization_barrier((left_own, arrived))
    chunks = stage(False, False, info, maps[:, 1], *rows, arrived, rights)
    lefts = over_op(left_late)
    arrived = exchange(chunks, 4 * count)
    chunks = stage(True, False, info, maps[:, 0], *cols, arrived, lefts)
    arrived = exchange(chunks, 4 * count)
    piece = stage(True, True, info, maps[:, 1], *rows, arrived, rights)
    pieces = copies_to(piece, "op", 4)
    return pieces.reshape(4, 2, 8, count * 64).swapaxes(0, 1).reshape(64, count * 64)


def solution(mesh):
    n_op, n_sec = mesh.devices.shape
    ny = 4
    nz = n_sec // (2 * ny)
    split = Mesh(mesh.devices.reshape(n_op, nz, ny, 2), ALL)
    placed = (
        P(None, SEC),
        P("op", SEC, None, None),
        P("op", SEC, None, None),
        P("op", None),
        P("op", None),
        P(),
        P(),
    )
    return jax.shard_map(
        functools.partial(on_device, (nz, ny)),
        mesh=split, in_specs=placed, out_specs=P(SEC, None), check_vma=False,
    )
```

```python
import functools

import jax
import jax.numpy as jnp
from jax import lax
from jax.experimental import pallas as pl
from jax.experimental.pallas import tpu as pltpu
from jax.sharding import Mesh
from jax.sharding import PartitionSpec as P


BF16, F32 = jnp.bfloat16, jnp.float32
NT = (((1,), (1,)), ((), ()))
SEC = ("z", "y", "c")
ALL = ("op",) + SEC


def iota(shape, axis):
    return lax.broadcasted_iota(jnp.int32, shape, axis)


def spot(info, sizes, sector):
    nz, ny = sizes
    core, rest = sector & 1, sector >> 1
    return ((core ^ info[2]) * ny + (rest & (ny - 1))) * nz + (rest >> (ny.bit_length() - 1))


def fold_out(out_ref, pair, count, first, second):
    for q in range(4):
        rows = jnp.concatenate([first[8 * q : 8 * q + 8], second[8 * q : 8 * q + 8]], axis=0)
        start = pl.multiple_of(q * count * 8 + pair * 16, 16)
        out_ref[pl.ds(start, 16), :] = rows.astype(BF16)


def pack(dense, start, value):
    dense[pl.ds(start, 32), :] = value
    dense[pl.ds(start + 32, 32), :] = pltpu.roll(value, 64, 1)


def send_packed(dense, out, owners):
    low = iota((16, 128), 1) < 64

    def narrow(step, carry):
        start = pl.multiple_of(step * 16, 16)
        even = dense[pl.ds(start * 2, 16, stride=2), :]
        odd = pltpu.roll(dense[pl.ds(start * 2 + 1, 16, stride=2), :], 64, 1)
        out[pl.ds(start, 16), :] = jnp.where(low, even, odd).astype(BF16)
        return carry

    lax.fori_loop(0, owners * 6 // 16, narrow, 0, unroll=16 if owners > 32 else 1)


def left_kernel(
    count, sizes, info, source, row_dims, col_dims, row_at, wave, env, out, blocks, dense
):
    lane = iota((64, 128), 1)
    low = lane < 64
    alive = iota((64, 128), 0) < col_dims[info[1]]

    def spread(pair, carry):
        value = wave[:, pl.ds(pl.multiple_of(pair * 128, 128), 128)].astype(F32)
        extent = jnp.where(low, row_dims[2 * pair], row_dims[2 * pair + 1] + 64)
        value = jnp.where(alive & (lane < extent), value, 0.0)
        turned = pltpu.roll(value, 64, 1)
        blocks[2 * pair] = jnp.where(low, value, turned).astype(BF16)
        blocks[2 * pair + 1] = jnp.where(low, turned, value).astype(BF16)
        return carry

    lax.fori_loop(0, count // 2, spread, 0, unroll=min(16, count // 2))
    zero = jnp.zeros((64, 128), BF16)

    def product(block):
        place = spot(info, sizes, block)
        e = env[pl.ds(pl.multiple_of(place * 32, 32), 32), :]
        f = blocks[source[block]]
        rhs = jnp.concatenate([jnp.where(low, f, zero), jnp.where(low, zero, f)], axis=0)
        return lax.dot_general(e, rhs, NT, preferred_element_type=F32)

    def group(step, carry):
        values = [product(step * 8 + i) for i in range(8)]
        for i in range(8):
            pack(dense, row_at[step * 8 + i], values[i])
        return carry

    lax.fori_loop(0, count // 8, group, 0, unroll=min(8, count // 8))
    send_packed(dense, out, count * 4)


def middle_kernel(
    count, sizes, turn, last, info, source, row_dims, col_dims, col_at,
    arrived, env_0, env_1, env_3, env_2a, env_2b, out, env, tiles, held, wide, dense, padded, offsets, sems,
):
    half_env = count * 16
    copies = [
        pltpu.make_async_copy(env_0, env.at[info[3]], sems.at[0]),
        pltpu.make_async_copy(env_1, env.at[info[4]], sems.at[1]),
        pltpu.make_async_copy(env_3, env.at[info[5]], sems.at[2]),
        pltpu.make_async_copy(env_2a, env.at[info[6], pl.ds(0, half_env)], sems.at[3]),
        pltpu.make_async_copy(env_2b, env.at[info[6], pl.ds(half_env, half_env)], sems.at[4]),
    ]
    for copy in copies:
        copy.start()
    lane8 = iota((8, 128), 1)
    low8 = lane8 < 64
    rows_in = 8 if last else 6
    total_rows = arrived.shape[0]

    def widen(step, carry):
        start = pl.multiple_of(step * 16, 16)
        wide[pl.ds(start, 16), :] = arrived[pl.ds(start, 16), :].astype(F32)
        return carry

    lax.fori_loop(0, total_rows // 16, widen, 0, unroll=16 if count > 8 else 1)
    wide[pl.ds(total_rows, 8), :] = jnp.zeros((8, 128), F32)


    def settle(w, block, value):
        turned = pltpu.roll(value, 64, 1)
        first, second = jnp.where(low8, value, turned), jnp.where(low8, turned, value)
        tiles[w, block] = jnp.concatenate([first, second], axis=0).astype(BF16)

    if turn:
        bit0, bit1 = (lane8 & 16) == 0, (lane8 & 32) == 0
        zero_tile = jnp.zeros((16, 128), BF16)
        for w in range(4):
            padded[w, count // 2] = zero_tile
        spot_of = iota((256, 128), 0)
        number = (spot_of >> 4) * 12 + (spot_of & 7) * 2 + ((spot_of >> 3) & 1)
        offsets[...] = jnp.where((spot_of & 7) < 6, number, -4096) - (iota((256, 128), 1) & 63)

        def regroup(e, carry):
            sets = []
            for k in range(2):
                got = [wide[pl.ds((8 * e + 4 * k + x) * rows_in, 8), :] for x in range(4)]
                for a, b in ((0, 1), (2, 3)):
                    one, two = got[a], got[b]
                    got[a] = jnp.where(bit0, one, pltpu.roll(two, 16, 1))
                    got[b] = jnp.where(bit0, pltpu.roll(one, 112, 1), two)
                for a, b in ((0, 2), (1, 3)):
                    one, two = got[a], got[b]
                    got[a] = jnp.where(bit1, one, pltpu.roll(two, 32, 1))
                    got[b] = jnp.where(bit1, pltpu.roll(one, 96, 1), two)
                sets.append(got)
            for w in range(4):
                one, two = sets[0][w], sets[1][w]
                first = jnp.where(low8, one, pltpu.roll(two, 64, 1))
                second = jnp.where(low8, pltpu.roll(one, 64, 1), two)
                padded[w, e] = jnp.concatenate([first, second], axis=0).astype(BF16)
            return carry

        lax.fori_loop(0, count // 2, regroup, 0, unroll=min(8, count // 2))
        lane_k = iota((256, 128), 1) & 63

        def place(block, carry):
            at = col_at[block]
            f = lax.div(at, 96)
            pick = (offsets[...] == at - f * 96) & (lane_k < col_dims[block])
            pick = jnp.where(pick, 1.0, 0.0).astype(BF16)
            lhs = [jnp.concatenate([padded[w, f], padded[w, f + 1]], axis=1) for w in range(4)]
            lhs = jnp.concatenate(lhs, axis=0)
            value = jnp.dot(lhs, pick, preferred_element_type=F32).astype(BF16)
            for w in range(4):
                tiles[w, block] = value[16 * w : 16 * w + 16]
            return carry
    else:

        def place(block, carry):
            for w in range(4):
                settle(w, block, wide[pl.ds((w * count + block) * rows_in, 8), :])
            return carry

    lax.fori_loop(0, count, place, 0, unroll=min(16, count))
    for copy in copies:
        copy.wait()

    low = iota((16, 128), 1) < 64
    zero = jnp.zeros((16, 128), BF16)
    pad = jnp.zeros((32, 96), F32)
    lane_in = iota((16, 128), 1) & 63
    if last:
        row = iota((16, 128), 0)
        natural = (row & 7) + (row >> 3) * 32 + info[0] * 8
        row_alive = natural < row_dims[info[1]]

    def env_of(block):
        start = pl.multiple_of(spot(info, sizes, block) * 32, 32)
        return jnp.concatenate([env[w, pl.ds(start, 32), :] for w in range(4)], axis=1)

    def summed(block):
        lhs = []
        for w in range(4):
            t = tiles[w, source[w, block]]
            lhs.append(jnp.concatenate([jnp.where(low, t, zero), jnp.where(low, zero, t)], axis=0))
        lhs = jnp.concatenate(lhs, axis=1)
        total = lax.dot_general(lhs, env_of(block), NT, preferred_element_type=F32)
        total = jnp.concatenate([total, pad], axis=1)
        total = total[:16] + pltpu.roll(total[16:], 32, 1)
        alive = lane_in < col_dims[block]
        return jnp.where(row_alive & alive if last else alive, total, 0.0)

    if last:

        def finish(pair, carry):
            value = summed(2 * pair) + pltpu.roll(summed(2 * pair + 1), 64, 1)
            out[:, pl.ds(pl.multiple_of(pair * 128, 128), 128)] = value.astype(BF16)
            return carry

        lax.fori_loop(0, count // 2, finish, 0, unroll=min(16, count // 2))
        return

    def keep(block, carry):
        value = summed(block)
        held[block] = (value + pltpu.roll(value, 64, 1)).astype(BF16)
        return carry

    lax.fori_loop(0, count, keep, 0, unroll=min(32, count))

    def product(block):
        slots = []
        for w in range(4):
            both = held[source[w, block]]
            rows = []
            for h in range(2):
                tile = jnp.where(low, both, zero) if h == 0 else jnp.where(low, zero, both)
                rows += [tile if v == w else zero for v in range(4)]
            slots.append(jnp.concatenate(rows, axis=0))
        rhs = jnp.concatenate(slots, axis=1)
        return lax.dot_general(env_of(block), rhs, NT, preferred_element_type=F32)

    if turn:

        def step(pair, carry):
            fold_out(out, pair, count, product(2 * pair), product(2 * pair + 1))
            return carry

        lax.fori_loop(0, count // 2, step, 0, unroll=min(16, count // 2))
        return

    def group(step, carry):
        values = [product(step * 8 + i) for i in range(8)]
        for i in range(8):
            pack(dense, col_at[step * 8 + i], values[i])
        return carry

    lax.fori_loop(0, count // 8, group, 0, unroll=min(8, count // 8))
    send_packed(dense, out, count * 4)


SMEM = pl.BlockSpec(memory_space=pltpu.SMEM)
VMEM = pl.BlockSpec(memory_space=pltpu.VMEM)
ANY = pl.BlockSpec(memory_space=pl.ANY)


def left_stage(count, sizes, info, source, row_dims, col_dims, row_at, wave, env):
    return pl.pallas_call(
        functools.partial(left_kernel, count, sizes),
        out_shape=jax.ShapeDtypeStruct((count * 24, 128), BF16),
        in_specs=[SMEM] * 5 + [VMEM] * 2,
        out_specs=VMEM,
        scratch_shapes=[
            pltpu.VMEM((count, 64, 128), BF16),
            pltpu.VMEM((count * 48 + 64, 128), F32),
        ],
        compiler_params=pltpu.CompilerParams(vmem_limit_bytes=20 * 2**20),
        cost_estimate=pl.CostEstimate(flops=count * 2**20, bytes_accessed=count * 24576, transcendentals=0),
        name="left_stage",
    )(info, source, row_dims, col_dims, row_at, wave, env)


def middle_stage(count, sizes, turn, last, info, source, row_dims, col_dims, col_at, arrived, envs):
    shape = (16, count * 64) if last else (count * (32 if turn else 24), 128)
    return pl.pallas_call(
        functools.partial(middle_kernel, count, sizes, turn, last),
        out_shape=jax.ShapeDtypeStruct(shape, BF16),
        in_specs=[SMEM] * 5 + [VMEM] + [ANY] * 5,
        out_specs=VMEM,
        scratch_shapes=[
            pltpu.VMEM((4, count * 32, 128), BF16),
            pltpu.VMEM((4, count, 16, 128), BF16),
            pltpu.VMEM((count, 16, 128), BF16),
            pltpu.VMEM((count * 32 + 8, 128), F32),
            pltpu.VMEM((count * 48 + 64, 128), F32),
            pltpu.VMEM((4, count // 2 + 1, 16, 128), BF16),
            pltpu.VMEM((256, 128), jnp.int32),
            pltpu.SemaphoreType.DMA((5,)),
        ],
        compiler_params=pltpu.CompilerParams(vmem_limit_bytes=26 * 2**20),
        cost_estimate=pl.CostEstimate(flops=count * 2**23, bytes_accessed=count * 49152, transcendentals=0),
        name="last_stage" if last else "middle_stage",
    )(info, source, row_dims, col_dims, col_at, arrived, *envs)


def fold(block):
    return jnp.concatenate([block[:32], block[32:]], axis=1)


def copies_to(value, axis, size):
    return lax.all_to_all(jnp.broadcast_to(value, (size,) + value.shape), axis, 0, 0, tiled=True)


def exchange(chunks, devices):
    shape = chunks.shape
    pieces = chunks.reshape(devices, shape[0] // devices // 2, 2, 128)
    return lax.all_to_all(pieces, ALL, 0, 0, tiled=True).reshape(shape)


def program(sizes, wave, left_env, right_env, left_map, right_map, left_dims, right_dims):
    nz, ny = sizes
    count = left_map.shape[1]
    me, core = lax.axis_index("op"), lax.axis_index("c")
    sector = lax.axis_index(SEC)
    shifts = (0, 1, 3, 2)
    starts = [jnp.cumsum(d) - d for d in (left_dims, right_dims)]
    info = jnp.stack([me, sector, core] + [lax.rem(me + 4 - s, 4) for s in shifts] + [me]).astype(jnp.int32)

    maps = copies_to(jnp.stack([left_map[0], right_map[0]]), "op", 4)
    own = jnp.stack([fold(left_env[0, 0]), fold(right_env[0, 0].T)])
    over_z = copies_to(own, "z", nz)
    over_y = copies_to(over_z, "y", ny)
    other = lax.ppermute(over_y, "c", [(0, 1), (1, 0)])

    def gathered(which):
        both = jnp.stack([over_y[:, :, which], other[:, :, which]])
        return both.reshape(count * 32, 128)

    left_own, right_own = gathered(0), gathered(1)

    def over_op(value):
        half = count * 16
        ahead = lax.ppermute(value, "op", [(i, (i + 1) % 4) for i in range(4)])
        behind = lax.ppermute(value, "op", [(i, (i + 3) % 4) for i in range(4)])
        far_a = lax.ppermute(ahead[:half], "op", [(i, (i + 1) % 4) for i in range(4)])
        far_b = lax.ppermute(behind[half:], "op", [(i, (i + 3) % 4) for i in range(4)])
        return [value, ahead, behind, far_a, far_b]

    stage = functools.partial(middle_stage, count, sizes)
    rows, cols = (left_dims, right_dims, starts[1]), (right_dims, left_dims, starts[0])
    rights = over_op(right_own)
    lefts = over_op(left_own)
    chunks = left_stage(
        count, sizes, info, left_map[0], left_dims, right_dims, starts[0], wave.T, left_own
    )
    arrived = exchange(chunks, 4 * count)
    chunks = stage(False, False, info, maps[:, 1], *rows, arrived, rights)
    arrived = exchange(chunks, 4 * count)
    chunks = stage(True, False, info, maps[:, 0], *cols, arrived, lefts)
    arrived = exchange(chunks, 4 * count)
    piece = stage(True, True, info, maps[:, 1], *rows, arrived, rights)
    pieces = copies_to(piece, "op", 4)
    return pieces.reshape(4, 2, 8, count * 64).swapaxes(0, 1).reshape(64, count * 64)


def solution(mesh):
    n_op, n_sec = mesh.devices.shape
    ny = 4
    nz = n_sec // (2 * ny)
    split = Mesh(mesh.devices.reshape(n_op, nz, ny, 2), ALL)
    placed = (
        P(None, SEC),
        P("op", SEC, None, None),
        P("op", SEC, None, None),
        P("op", None),
        P("op", None),
        P(),
        P(),
    )
    return jax.shard_map(
        functools.partial(program, (nz, ny)),
        mesh=split, in_specs=placed, out_specs=P(SEC, None), check_vma=False,
    )
```

```python
import functools

import jax
import jax.numpy as jnp
from jax import lax
from jax.experimental import pallas as pl
from jax.experimental.pallas import tpu as pltpu
from jax.sharding import Mesh
from jax.sharding import PartitionSpec as P


BF16, F32 = jnp.bfloat16, jnp.float32
NT = (((1,), (1,)), ((), ()))
SEC = ("z", "y", "c")
ALL = ("op",) + SEC


def iota(shape, axis):
    return lax.broadcasted_iota(jnp.int32, shape, axis)


def spot(info, sizes, sector):
    nz, ny = sizes
    core, rest = sector & 1, sector >> 1
    return ((core ^ info[2]) * ny + (rest & (ny - 1))) * nz + (rest >> (ny.bit_length() - 1))


def fold_out(out_ref, pair, count, first, second):
    for q in range(4):
        rows = jnp.concatenate([first[8 * q : 8 * q + 8], second[8 * q : 8 * q + 8]], axis=0)
        start = pl.multiple_of(q * count * 8 + pair * 16, 16)
        out_ref[pl.ds(start, 16), :] = rows.astype(BF16)


def pack(dense, start, value):
    dense[pl.ds(start, 32), :] = value
    dense[pl.ds(start + 32, 32), :] = pltpu.roll(value, 64, 1)


def send_packed(dense, out, owners):
    low = iota((16, 128), 1) < 64

    def narrow(step, carry):
        start = pl.multiple_of(step * 16, 16)
        even = dense[pl.ds(start * 2, 16, stride=2), :]
        odd = pltpu.roll(dense[pl.ds(start * 2 + 1, 16, stride=2), :], 64, 1)
        out[pl.ds(start, 16), :] = jnp.where(low, even, odd).astype(BF16)
        return carry

    lax.fori_loop(0, owners * 6 // 16, narrow, 0, unroll=16 if owners > 32 else 1)


def left_kernel(
    count, sizes, info, source, row_dims, col_dims, row_at, wave, env, out, blocks, dense
):
    lane = iota((64, 128), 1)
    low = lane < 64
    alive = iota((64, 128), 0) < col_dims[info[1]]

    def spread(pair, carry):
        value = wave[:, pl.ds(pl.multiple_of(pair * 128, 128), 128)].astype(F32)
        extent = jnp.where(low, row_dims[2 * pair], row_dims[2 * pair + 1] + 64)
        value = jnp.where(alive & (lane < extent), value, 0.0)
        turned = pltpu.roll(value, 64, 1)
        blocks[2 * pair] = jnp.where(low, value, turned).astype(BF16)
        blocks[2 * pair + 1] = jnp.where(low, turned, value).astype(BF16)
        return carry

    lax.fori_loop(0, count // 2, spread, 0, unroll=min(16, count // 2))
    zero = jnp.zeros((64, 128), BF16)

    def product(block):
        place = spot(info, sizes, block)
        e = env[pl.ds(pl.multiple_of(place * 32, 32), 32), :]
        f = blocks[source[block]]
        rhs = jnp.concatenate([jnp.where(low, f, zero), jnp.where(low, zero, f)], axis=0)
        return lax.dot_general(e, rhs, NT, preferred_element_type=F32)

    def group(step, carry):
        values = [product(step * 8 + i) for i in range(8)]
        for i in range(8):
            pack(dense, row_at[step * 8 + i], values[i])
        return carry

    lax.fori_loop(0, count // 8, group, 0, unroll=min(8, count // 8))
    send_packed(dense, out, count * 4)


def middle_kernel(
    count, sizes, turn, last, info, source, row_dims, col_dims, col_at,
    arrived, env_0, env_1, env_3, env_2a, env_2b, out, env, tiles, held, wide, dense, padded, offsets, sems,
):
    half_env = count * 16
    copies = [
        pltpu.make_async_copy(env_0, env.at[info[3]], sems.at[0]),
        pltpu.make_async_copy(env_1, env.at[info[4]], sems.at[1]),
        pltpu.make_async_copy(env_3, env.at[info[5]], sems.at[2]),
        pltpu.make_async_copy(env_2a, env.at[info[6], pl.ds(0, half_env)], sems.at[3]),
        pltpu.make_async_copy(env_2b, env.at[info[6], pl.ds(half_env, half_env)], sems.at[4]),
    ]
    for copy in copies:
        copy.start()
    lane8 = iota((8, 128), 1)
    low8 = lane8 < 64
    rows_in = 8 if last else 6
    total_rows = arrived.shape[0]

    def widen(step, carry):
        start = pl.multiple_of(step * 16, 16)
        wide[pl.ds(start, 16), :] = arrived[pl.ds(start, 16), :].astype(F32)
        return carry

    lax.fori_loop(0, total_rows // 16, widen, 0, unroll=16 if count > 8 else 1)
    wide[pl.ds(total_rows, 8), :] = jnp.zeros((8, 128), F32)


    def settle(w, block, value):
        turned = pltpu.roll(value, 64, 1)
        first, second = jnp.where(low8, value, turned), jnp.where(low8, turned, value)
        tiles[w, block] = jnp.concatenate([first, second], axis=0).astype(BF16)

    if turn:
        bit0, bit1 = (lane8 & 16) == 0, (lane8 & 32) == 0
        zero_tile = jnp.zeros((16, 128), BF16)
        for w in range(4):
            padded[w, count // 2] = zero_tile
        spot_of = iota((256, 128), 0)
        number = (spot_of >> 4) * 12 + (spot_of & 7) * 2 + ((spot_of >> 3) & 1)
        offsets[...] = jnp.where((spot_of & 7) < 6, number, -4096) - (iota((256, 128), 1) & 63)

        def regroup(e, carry):
            sets = []
            for k in range(2):
                got = [wide[pl.ds((8 * e + 4 * k + x) * rows_in, 8), :] for x in range(4)]
                for a, b in ((0, 1), (2, 3)):
                    one, two = got[a], got[b]
                    got[a] = jnp.where(bit0, one, pltpu.roll(two, 16, 1))
                    got[b] = jnp.where(bit0, pltpu.roll(one, 112, 1), two)
                for a, b in ((0, 2), (1, 3)):
                    one, two = got[a], got[b]
                    got[a] = jnp.where(bit1, one, pltpu.roll(two, 32, 1))
                    got[b] = jnp.where(bit1, pltpu.roll(one, 96, 1), two)
                sets.append(got)
            for w in range(4):
                one, two = sets[0][w], sets[1][w]
                first = jnp.where(low8, one, pltpu.roll(two, 64, 1))
                second = jnp.where(low8, pltpu.roll(one, 64, 1), two)
                padded[w, e] = jnp.concatenate([first, second], axis=0).astype(BF16)
            return carry

        lax.fori_loop(0, count // 2, regroup, 0, unroll=min(8, count // 2))
        lane_k = iota((256, 128), 1) & 63

        def place(block, carry):
            at = col_at[block]
            f = lax.div(at, 96)
            pick = (offsets[...] == at - f * 96) & (lane_k < col_dims[block])
            pick = jnp.where(pick, 1.0, 0.0).astype(BF16)
            lhs = [jnp.concatenate([padded[w, f], padded[w, f + 1]], axis=1) for w in range(4)]
            lhs = jnp.concatenate(lhs, axis=0)
            value = jnp.dot(lhs, pick, preferred_element_type=F32).astype(BF16)
            for w in range(4):
                tiles[w, block] = value[16 * w : 16 * w + 16]
            return carry
    else:

        def place(block, carry):
            for w in range(4):
                settle(w, block, wide[pl.ds((w * count + block) * rows_in, 8), :])
            return carry

    lax.fori_loop(0, count, place, 0, unroll=min(16, count))
    for copy in copies:
        copy.wait()

    low = iota((16, 128), 1) < 64
    zero = jnp.zeros((16, 128), BF16)
    pad = jnp.zeros((32, 96), F32)
    lane_in = iota((16, 128), 1) & 63
    if last:
        row = iota((16, 128), 0)
        natural = (row & 7) + (row >> 3) * 32 + info[0] * 8
        row_alive = natural < row_dims[info[1]]

    def env_of(block):
        start = pl.multiple_of(spot(info, sizes, block) * 32, 32)
        return jnp.concatenate([env[w, pl.ds(start, 32), :] for w in range(4)], axis=1)

    def summed(block):
        lhs = []
        for w in range(4):
            t = tiles[w, source[(info[0] - w) & 3, block]]
            lhs.append(jnp.concatenate([jnp.where(low, t, zero), jnp.where(low, zero, t)], axis=0))
        lhs = jnp.concatenate(lhs, axis=1)
        total = lax.dot_general(lhs, env_of(block), NT, preferred_element_type=F32)
        total = jnp.concatenate([total, pad], axis=1)
        total = total[:16] + pltpu.roll(total[16:], 32, 1)
        alive = lane_in < col_dims[block]
        return jnp.where(row_alive & alive if last else alive, total, 0.0)

    if last:

        def finish(pair, carry):
            value = summed(2 * pair) + pltpu.roll(summed(2 * pair + 1), 64, 1)
            out[:, pl.ds(pl.multiple_of(pair * 128, 128), 128)] = value.astype(BF16)
            return carry

        lax.fori_loop(0, count // 2, finish, 0, unroll=min(16, count // 2))
        return

    def keep(block, carry):
        value = summed(block)
        held[block] = (value + pltpu.roll(value, 64, 1)).astype(BF16)
        return carry

    lax.fori_loop(0, count, keep, 0, unroll=min(32, count))

    def product(block):
        slots = []
        for w in range(4):
            both = held[source[(info[0] - w) & 3, block]]
            rows = []
            for h in range(2):
                tile = jnp.where(low, both, zero) if h == 0 else jnp.where(low, zero, both)
                rows += [tile if v == w else zero for v in range(4)]
            slots.append(jnp.concatenate(rows, axis=0))
        rhs = jnp.concatenate(slots, axis=1)
        return lax.dot_general(env_of(block), rhs, NT, preferred_element_type=F32)

    if turn:

        def step(pair, carry):
            fold_out(out, pair, count, product(2 * pair), product(2 * pair + 1))
            return carry

        lax.fori_loop(0, count // 2, step, 0, unroll=min(16, count // 2))
        return

    def group(step, carry):
        values = [product(step * 8 + i) for i in range(8)]
        for i in range(8):
            pack(dense, col_at[step * 8 + i], values[i])
        return carry

    lax.fori_loop(0, count // 8, group, 0, unroll=min(8, count // 8))
    send_packed(dense, out, count * 4)


SMEM = pl.BlockSpec(memory_space=pltpu.SMEM)
VMEM = pl.BlockSpec(memory_space=pltpu.VMEM)
ANY = pl.BlockSpec(memory_space=pl.ANY)


def left_stage(count, sizes, info, source, row_dims, col_dims, row_at, wave, env):
    return pl.pallas_call(
        functools.partial(left_kernel, count, sizes),
        out_shape=jax.ShapeDtypeStruct((count * 24, 128), BF16),
        in_specs=[SMEM] * 5 + [VMEM] * 2,
        out_specs=VMEM,
        scratch_shapes=[
            pltpu.VMEM((count, 64, 128), BF16),
            pltpu.VMEM((count * 48 + 64, 128), F32),
        ],
        compiler_params=pltpu.CompilerParams(vmem_limit_bytes=20 * 2**20),
        cost_estimate=pl.CostEstimate(flops=count * 2**20, bytes_accessed=count * 24576, transcendentals=0),
        name="left_stage",
    )(info, source, row_dims, col_dims, row_at, wave, env)


def middle_stage(count, sizes, turn, last, info, source, row_dims, col_dims, col_at, arrived, envs):
    shape = (16, count * 64) if last else (count * (32 if turn else 24), 128)
    return pl.pallas_call(
        functools.partial(middle_kernel, count, sizes, turn, last),
        out_shape=jax.ShapeDtypeStruct(shape, BF16),
        in_specs=[SMEM] * 5 + [VMEM] + [ANY] * 5,
        out_specs=VMEM,
        scratch_shapes=[
            pltpu.VMEM((4, count * 32, 128), BF16),
            pltpu.VMEM((4, count, 16, 128), BF16),
            pltpu.VMEM((count, 16, 128), BF16),
            pltpu.VMEM((count * 32 + 8, 128), F32),
            pltpu.VMEM((count * 48 + 64, 128), F32),
            pltpu.VMEM((4, count // 2 + 1, 16, 128), BF16),
            pltpu.VMEM((256, 128), jnp.int32),
            pltpu.SemaphoreType.DMA((5,)),
        ],
        compiler_params=pltpu.CompilerParams(vmem_limit_bytes=26 * 2**20),
        cost_estimate=pl.CostEstimate(flops=count * 2**23, bytes_accessed=count * 49152, transcendentals=0),
        name="last_stage" if last else "middle_stage",
    )(info, source, row_dims, col_dims, col_at, arrived, *envs)


def fold(block):
    return jnp.concatenate([block[:32], block[32:]], axis=1)


def copies_to(value, axis, size):
    return lax.all_to_all(jnp.broadcast_to(value, (size,) + value.shape), axis, 0, 0, tiled=True)


def exchange(chunks, devices):
    shape = chunks.shape
    pieces = chunks.reshape(devices, shape[0] // devices // 2, 2, 128)
    return lax.all_to_all(pieces, ALL, 0, 0, tiled=True).reshape(shape)


def program(sizes, wave, left_env, right_env, left_map, right_map, left_dims, right_dims):
    nz, ny = sizes
    count = left_map.shape[1]
    me, core = lax.axis_index("op"), lax.axis_index("c")
    sector = lax.axis_index(SEC)
    shifts = (0, 1, 3, 2)
    starts = [jnp.cumsum(d) - d for d in (left_dims, right_dims)]
    info = jnp.stack([me, sector, core] + [lax.rem(me + 4 - s, 4) for s in shifts] + [me]).astype(jnp.int32)

    own = jnp.stack([fold(left_env[0, 0]), fold(right_env[0, 0].T)])
    over_z = copies_to(own, "z", nz)
    over_y = copies_to(over_z, "y", ny)
    other = lax.ppermute(over_y, "c", [(0, 1), (1, 0)])

    def gathered(which):
        both = jnp.stack([over_y[:, :, which], other[:, :, which]])
        return both.reshape(count * 32, 128)

    left_own, right_own = gathered(0), gathered(1)

    def over_op(value):
        half = count * 16
        ahead = lax.ppermute(value, "op", [(i, (i + 1) % 4) for i in range(4)])
        behind = lax.ppermute(value, "op", [(i, (i + 3) % 4) for i in range(4)])
        far_a = lax.ppermute(ahead[:half], "op", [(i, (i + 1) % 4) for i in range(4)])
        far_b = lax.ppermute(behind[half:], "op", [(i, (i + 3) % 4) for i in range(4)])
        return [value, ahead, behind, far_a, far_b]

    stage = functools.partial(middle_stage, count, sizes)
    rows, cols = (left_dims, right_dims, starts[1]), (right_dims, left_dims, starts[0])
    rights = over_op(right_own)
    lefts = over_op(left_own)
    chunks = left_stage(
        count, sizes, info, left_map[0], left_dims, right_dims, starts[0], wave.T, left_own
    )
    own_maps, chunks = lax.optimization_barrier((jnp.stack([left_map[0], right_map[0]]), chunks))
    others = [lax.ppermute(own_maps, "op", [(i, (i + k) % 4) for i in range(4)]) for k in (1, 2, 3)]
    maps = jnp.stack([own_maps] + others)
    arrived = exchange(chunks, 4 * count)
    chunks = stage(False, False, info, maps[:, 1], *rows, arrived, rights)
    arrived = exchange(chunks, 4 * count)
    chunks = stage(True, False, info, maps[:, 0], *cols, arrived, lefts)
    arrived = exchange(chunks, 4 * count)
    piece = stage(True, True, info, maps[:, 1], *rows, arrived, rights)
    pieces = copies_to(piece, "op", 4)
    return pieces.reshape(4, 2, 8, count * 64).swapaxes(0, 1).reshape(64, count * 64)


def solution(mesh):
    n_op, n_sec = mesh.devices.shape
    ny = 4
    nz = n_sec // (2 * ny)
    split = Mesh(mesh.devices.reshape(n_op, nz, ny, 2), ALL)
    placed = (
        P(None, SEC),
        P("op", SEC, None, None),
        P("op", SEC, None, None),
        P("op", None),
        P("op", None),
        P(),
        P(),
    )
    return jax.shard_map(
        functools.partial(program, (nz, ny)),
        mesh=split, in_specs=placed, out_specs=P(SEC, None), check_vma=False,
    )
```
